32 devices in a mesh: groups: 2 (over x), azim: 16 (over z, y, core).
Axes of the slice: x: 2, y: 2, z: 4, core: 2. Of those that a mesh axis runs over, the one named last changes fastest.
Arguments:
- conserved: float32 [5, 256, 2048], P(None, ('groups', 'azim')), parts along dimension 1, may hold values from -6 to 6
- velocity: float32 [256, 2048], P(('groups', 'azim')), parts along dimension 0, may hold values from -0.8 to 0.8
- viscosity: float32 [5], replicated, may hold values from 0.02 to 0.1
- shifts: int32 [4, 64], P('groups'), parts along dimension 0, may hold values from 0 to 127
Outputs:
- advanced: float32 [5, 256, 2048], P(None, ('groups', 'azim')), parts along dimension 1
The draws below stay inside these ranges and needn't reach their ends.
There are 2 independent parts, one for each index of `groups`. The reference program is written for one: setup_inputs(seed, part) draws one part's arguments, and reference() takes and returns one part's arrays. A program takes and returns all parts, laid end to end along the dimension named above; an argument that names none is the same for every part. Nothing has to cross between parts.
All inputs are finite; a program needn't handle non-finite values.
Results may differ from the reference program's by a relative error of at most 0.0003.
Values sent between devices are 32-bit elements; how exact they have to be, the bound alone decides.
A program may use at most 64 MiB of HBM per device.

```python
import math
import jax
import jax.numpy as jnp

NR = 64
FIELDS = 5
STEPS = 2
NPHI = 128
COLS = 2048


def place_ends(array, key, low, high):
    longest = array.shape.index(max(array.shape))
    spots = []
    for shift in (0, 1):
        where = [jax.random.randint(jax.random.fold_in(key, axis), (), 0, length) for axis, length in enumerate(array.shape)]
        where[longest] = (where[longest] + shift) % array.shape[longest]
        spots.append(tuple(where))
    return array.at[spots[0]].set(low).at[spots[1]].set(high)


def levels(stream_key, dims, split, smallest, top_value):
    def one(axis_at, shards_of):
        steps = jax.random.uniform(jax.random.fold_in(jax.random.fold_in(stream_key, 6), axis_at), (shards_of,), jnp.float32, smallest / len(split), top_value / len(split))
        return jnp.repeat(jnp.exp(steps), dims[axis_at] // shards_of).reshape((-1,) + (1,) * (len(dims) - axis_at - 1))

    loudness = one(*split[0])
    for cut in split[1:]:
        loudness = loudness * one(*cut)
    return loudness


def normal_values(stream_key, dims, scale, bound, split=(), kind=jnp.bfloat16):
    drawn = scale * jax.random.normal(stream_key, dims, jnp.float32)
    if split:
        drawn = drawn * levels(stream_key, dims, split, -0.22, 0.18)
    return jnp.clip(drawn, -bound, bound).astype(kind)


def setup_inputs(seed: int = 0, part: int = 0) -> dict:
    keys = jax.random.split(jax.random.key(seed), 5)
    part_keys = jax.random.split(jax.random.fold_in(keys[4], part), 5)
    conserved = normal_values(part_keys[0], (FIELDS, NPHI, COLS), 1.0, 6.0, ((1, 16),), jnp.float32)
    velocity = jnp.clip(jax.random.uniform(part_keys[1], (NPHI, COLS), jnp.float32, -0.8, 0.8) * levels(part_keys[1], (NPHI, COLS), ((0, 16),), -0.4, 0.0), -0.8, 0.8)
    viscosity = jnp.clip(jnp.exp(jax.random.uniform(keys[2], (FIELDS,), jnp.float32, math.log(0.02), math.log(0.1))), 0.02, 0.1)
    shifts = place_ends(jax.random.randint(part_keys[3], (STEPS, NR), 0, NPHI), jax.random.fold_in(part_keys[3], 1), 0, NPHI - 1).astype(jnp.int32)
    return dict(conserved=conserved, velocity=velocity, viscosity=viscosity, shifts=shifts)


def minmod(left, right):
    return 0.5 * (jnp.sign(left) + jnp.sign(right)) * jnp.minimum(jnp.abs(left), jnp.abs(right))


def lateral_sum(inner, heights):
    width = inner.shape[2]
    height_of = jnp.arange(width, dtype=jnp.int32) % heights
    outward = jnp.concatenate([inner[:, :, heights:], inner[:, :, width - heights:]], axis=2)
    inward = jnp.concatenate([inner[:, :, :heights], inner[:, :, :width - heights]], axis=2)
    upper = jnp.concatenate([inner[:, :, 1:], inner[:, :, width - 1:]], axis=2)
    upper = jnp.where((height_of == heights - 1)[None, None, :], inner, upper)
    lower = jnp.concatenate([inner[:, :, :1], inner[:, :, :width - 1]], axis=2)
    lower = jnp.where((height_of == 0)[None, None, :], inner, lower)
    return outward + inward + upper + lower - 4.0 * inner


def tendency(ext, speed, viscosity, heights):
    count = ext.shape[1]
    diff = ext[:, 1:] - ext[:, :-1]
    slope = minmod(diff[:, :-1], diff[:, 1:])
    left_state = ext[:, 1:count - 2] + 0.5 * slope[:, 0:count - 3]
    right_state = ext[:, 2:count - 1] - 0.5 * slope[:, 1:count - 2]
    face_speed = 0.5 * (speed[1:count - 2] + speed[2:count - 1])
    flux = jnp.maximum(face_speed, 0.0) * left_state + jnp.minimum(face_speed, 0.0) * right_state
    inner = ext[:, 2:count - 2]
    azimuthal = ext[:, 3:count - 1] + ext[:, 1:count - 3] - 2.0 * inner
    lateral = lateral_sum(inner, heights)
    return -(flux[:, 1:] - flux[:, :-1]) + viscosity[:, None, None] * (azimuthal + lateral)


def wrapped(field, width):
    return jnp.concatenate([field[:, -width:], field, field[:, :width]], axis=1)


def reference(conserved, velocity, viscosity, shifts):
    state = conserved
    speed = jnp.concatenate([velocity[-2:], velocity, velocity[:2]], axis=0)
    total = state.shape[1]
    width = state.shape[2]
    heights = width // shifts.shape[1]
    for step in range(STEPS):
        first = state + tendency(wrapped(state, 2), speed, viscosity, heights)
        second = 0.75 * state + 0.25 * (first + tendency(wrapped(first, 2), speed, viscosity, heights))
        third = (1.0 / 3.0) * state + (2.0 / 3.0) * (second + tendency(wrapped(second, 2), speed, viscosity, heights))
        per_column = jnp.repeat(shifts[step], heights)
        anchor = jnp.mod(jnp.arange(total, dtype=jnp.int32)[:, None] - per_column[None, :], total).astype(jnp.int32)
        anchor = jnp.broadcast_to(anchor[None], third.shape)
        state = jnp.take_along_axis(third, anchor, axis=1)
    return state
```

```python
import functools

import jax
import jax.numpy as jnp
from jax import lax
from jax.experimental import pallas as pl
from jax.experimental.pallas import tpu as pltpu
from jax.sharding import PartitionSpec as P

STEPS = 2
HALO = 3
LANES = 128
SUBLANES = 8


def padded(cells, sides, width):
    for axis, dim in sides:
        count = lax.axis_size(axis)
        head = lax.slice_in_dim(cells, 0, width, axis=dim)
        tail = lax.slice_in_dim(cells, cells.shape[dim] - width, cells.shape[dim], axis=dim)
        cells = jnp.concatenate(
            [
                lax.ppermute(tail, axis, [(i, (i + 1) % count) for i in range(count)]),
                cells,
                lax.ppermute(head, axis, [((i + 1) % count, i) for i in range(count)]),
            ],
            axis=dim,
        )
    return cells


def shifted(value, axis, steps):
    count = lax.axis_size(axis)
    pairs = [(source, (source + steps) % count) for source in range(count)]
    return lax.ppermute(value, axis, pairs)


def minmod(left, right):
    return 0.5 * (jnp.sign(left) + jnp.sign(right)) * jnp.minimum(jnp.abs(left), jnp.abs(right))


def lateral_sum(inner, heights):
    width = inner.shape[2]
    height_of = jnp.arange(width, dtype=jnp.int32) % heights
    outward = jnp.concatenate([inner[:, :, heights:], inner[:, :, width - heights :]], axis=2)
    inward = jnp.concatenate([inner[:, :, :heights], inner[:, :, : width - heights]], axis=2)
    upper = jnp.concatenate([inner[:, :, 1:], inner[:, :, width - 1 :]], axis=2)
    upper = jnp.where((height_of == heights - 1)[None, None, :], inner, upper)
    lower = jnp.concatenate([inner[:, :, :1], inner[:, :, : width - 1]], axis=2)
    lower = jnp.where((height_of == 0)[None, None, :], inner, lower)
    return outward + inward + upper + lower - 4.0 * inner


def tendency(ext, speed, viscosity, heights):
    count = ext.shape[1]
    diff = ext[:, 1:] - ext[:, :-1]
    slope = minmod(diff[:, :-1], diff[:, 1:])
    left_state = ext[:, 1 : count - 2] + 0.5 * slope[:, 0 : count - 3]
    right_state = ext[:, 2 : count - 1] - 0.5 * slope[:, 1 : count - 2]
    face_speed = 0.5 * (speed[1 : count - 2] + speed[2 : count - 1])
    flux = jnp.maximum(face_speed, 0.0) * left_state + jnp.minimum(face_speed, 0.0) * right_state
    inner = ext[:, 2 : count - 2]
    azimuthal = ext[:, 3 : count - 1] + ext[:, 1 : count - 3] - 2.0 * inner
    lateral = lateral_sum(inner, heights)
    return -(flux[:, 1:] - flux[:, :-1]) + viscosity[:, None, None] * (azimuthal + lateral)


def section_rim(field):
    return padded(field, (("azim", 1),), 2)


def slide_down(joined, amount, limit):
    current = joined
    level = 0
    while 1 << level < limit:
        stride = 1 << level
        taken = amount >> level & 1 == 1
        moved = jnp.concatenate(
            [jnp.zeros_like(current[:, :stride]), current[:, : current.shape[1] - stride]], axis=1
        )
        current = jnp.where(taken[None, None, :], moved, current)
        level = level + 1
    return current


def by_azimuth(conserved, velocity, viscosity, shifts):
    state = conserved
    block = state.shape[1]
    heights = state.shape[2] // shifts.shape[1]
    devices = lax.axis_size("azim")
    levels = devices.bit_length() - 1
    speed_wide = padded(velocity, (("azim", 0),), 6)
    speed_near = speed_wide[4:-4]
    for step in range(STEPS):
        first = state + tendency(section_rim(state), speed_near, viscosity, heights)
        second = 0.75 * state + 0.25 * (
            first + tendency(section_rim(first), speed_near, viscosity, heights)
        )
        third = 1.0 / 3.0 * state + 2.0 / 3.0 * (
            second + tendency(section_rim(second), speed_near, viscosity, heights)
        )
        per_column = jnp.repeat(shifts[step], heights)
        whole_blocks = per_column // block
        remainder = per_column - whole_blocks * block
        moved = third
        for level in range(levels):
            taken = whole_blocks >> level & 1 == 1
            arrived = shifted(moved, "azim", 1 << level)
            moved = jnp.where(taken[None, None, :], arrived, moved)
        preceding = shifted(moved, "azim", 1)
        joined = jnp.concatenate([preceding, moved], axis=1)
        state = slide_down(joined, remainder, block)[:, block:]
    return state


def disc_kernel(
    n,
    heights,
    cons,
    vel,
    visc,
    shifts,
    out,
    ubuf,
    u,
    vp,
    vn,
    t1,
    t2,
    obuf,
    a_send,
    a_recv,
    v_send,
    v_recv,
    h_send,
    h_recv,
    o_send,
    o_recv,
    own_sem,
):
    fields, block, cols = cons.shape
    width = cols // n
    owned = width // heights
    azim = n * block
    rim = HALO * heights
    me = lax.axis_index("azim")

    barrier = pltpu.get_barrier_semaphore()

    def greet(k, carry):
        pl.semaphore_signal(barrier, inc=1, device_id={"azim": lax.rem(me + k, n)})
        return carry

    lax.fori_loop(1, n, greet, 0)
    pl.semaphore_wait(barrier, n - 1)

    def lanes(d):
        return pl.ds(pl.multiple_of(d * width, width), width)

    def rows(d):
        return pl.ds(pl.multiple_of(d * block, block), block)

    def send_in(k):
        to = lax.rem(me + k, n)
        return (
            pltpu.make_async_remote_copy(
                src_ref=vel.at[:, lanes(to)],
                dst_ref=ubuf.at[fields, rows(me), :],
                send_sem=v_send.at[k],
                recv_sem=v_recv.at[k],
                device_id={"azim": to},
            ),
            pltpu.make_async_remote_copy(
                src_ref=cons.at[:, :, lanes(to)],
                dst_ref=ubuf.at[pl.ds(0, fields), rows(me), :],
                send_sem=a_send.at[k],
                recv_sem=a_recv.at[k],
                device_id={"azim": to},
            ),
        )

    def start_in(k, carry):
        for copy in send_in(k):
            copy.start()
        return carry

    lax.fori_loop(1, n, start_in, 0)
    own_v = pltpu.make_async_copy(vel.at[:, lanes(me)], ubuf.at[fields, rows(me), :], own_sem.at[0])
    own_u = pltpu.make_async_copy(
        cons.at[:, :, lanes(me)], ubuf.at[pl.ds(0, fields), rows(me), :], own_sem.at[1]
    )
    own_v.start()
    own_u.start()
    own_v.wait()
    own_u.wait()

    def wait_in(k, carry):
        source = lax.rem(me + n - k, n)
        for copy in send_in(k):
            copy.wait_send()
        pltpu.make_async_remote_copy(
            src_ref=vel.at[:, lanes(source)],
            dst_ref=ubuf.at[fields, rows(source), :],
            send_sem=v_send.at[k],
            recv_sem=v_recv.at[k],
            device_id={"azim": source},
        ).wait_recv()
        pltpu.make_async_remote_copy(
            src_ref=cons.at[:, :, lanes(source)],
            dst_ref=ubuf.at[pl.ds(0, fields), rows(source), :],
            send_sem=a_send.at[k],
            recv_sem=a_recv.at[k],
            device_id={"azim": source},
        ).wait_recv()
        return carry

    lax.fori_loop(1, n, wait_in, 0)

    def turn(f, carry):
        u[0, f, rim : rim + width, :] = ubuf[f].T
        return carry

    lax.fori_loop(0, fields + 1, turn, 0)

    def halo(step, planes):
        inner = pltpu.make_async_remote_copy(
            src_ref=u.at[step, pl.ds(0, planes), pl.ds(rim, rim), :],
            dst_ref=u.at[step, pl.ds(0, planes), pl.ds(rim + width, rim), :],
            send_sem=h_send.at[step, 0],
            recv_sem=h_recv.at[step, 0],
            device_id={"azim": lax.rem(me + n - 1, n)},
        )
        outer = pltpu.make_async_remote_copy(
            src_ref=u.at[step, pl.ds(0, planes), pl.ds(width, rim), :],
            dst_ref=u.at[step, pl.ds(0, planes), pl.ds(0, rim), :],
            send_sem=h_send.at[step, 1],
            recv_sem=h_recv.at[step, 1],
            device_id={"azim": lax.rem(me + 1, n)},
        )

        @pl.when(me > 0)
        def _():
            inner.start()

        @pl.when(me < n - 1)
        def _():
            outer.start()

        @pl.when(me > 0)
        def _():
            inner.wait_send()
            outer.wait_recv()

        @pl.when(me < n - 1)
        def _():
            outer.wait_send()
            inner.wait_recv()

    top = lax.broadcasted_iota(jnp.int32, (heights, azim), 0) == heights - 1
    radii = owned + 2 * HALO

    def part(r):
        return slice(r * heights, (r + 1) * heights)

    def stage(load, nu, first, last, write):
        here = load(first)
        below = here - load(first - 1)
        if first == HALO:
            below = jnp.where(me == 0, 0.0, below)
        for r in range(first, last):
            after = load(r + 1)
            above = after - here
            if r + 1 == HALO:
                above = jnp.where(me == 0, 0.0, above)
            if r + 1 == HALO + owned:
                above = jnp.where(me == n - 1, 0.0, above)
            x = here
            d = x - pltpu.roll(x, 1, 1)
            dp = pltpu.roll(d, azim - 1, 1)
            low = jnp.minimum(d, dp)
            high = jnp.maximum(d, dp)
            half = 0.5 * (jnp.maximum(low, 0.0) + jnp.minimum(high, 0.0))
            p = vp[part(r), :] * (x + half)
            q = vn[part(r), :] * (x - half)
            change = (p - q) + (pltpu.roll(q, azim - 1, 1) - pltpu.roll(p, 1, 1))
            e = jnp.where(top, 0.0, pltpu.roll(x, heights - 1, 0) - x)
            spread = (dp - d) + (e - pltpu.roll(e, 1, 0)) + (above - below)
            write(r, x, nu * spread - change)
            here = after
            below = above

    for step in range(STEPS):
        halo(step, fields + 1 if step == 0 else fields)
        if step == 0:
            for r in range(1, radii - 1):
                v = u[0, fields, part(r), :]
                speed = 0.5 * (v + pltpu.roll(v, 1, 1))
                vn[part(r), :] = jnp.minimum(speed, 0.0)
                vp[part(r), :] = pltpu.roll(jnp.maximum(speed, 0.0), azim - 1, 1)

        def advance(f, carry):
            nu = visc[f]

            def write1(r, x, change):
                t1[part(r), :] = x + change

            def write2(r, x, change):
                t2[part(r), :] = 0.75 * u[step, f, part(r), :] + 0.25 * (x + change)

            def write3(r, x, change):
                y = (1.0 / 3.0) * u[step, f, part(r), :] + (2.0 / 3.0) * (x + change)
                amount = shifts[step, me * owned + (r - HALO)]
                y = pltpu.roll(y, amount, 1)
                if step + 1 < STEPS:
                    u[step + 1, f, part(r), :] = y
                else:
                    t1[part(r), :] = y

            stage(lambda r: u[step, f, part(r), :], nu, 1, radii - 1, write1)
            stage(lambda r: t1[part(r), :], nu, 2, radii - 2, write2)
            stage(lambda r: t2[part(r), :], nu, 3, radii - 3, write3)
            if step + 1 == STEPS:
                obuf[f] = t1[rim : rim + width, :].T
            return carry

        lax.fori_loop(0, fields, advance, 0)

    def send_out(k):
        to = lax.rem(me + k, n)
        return pltpu.make_async_remote_copy(
            src_ref=obuf.at[:, rows(to), :],
            dst_ref=out.at[:, :, lanes(me)],
            send_sem=o_send.at[k],
            recv_sem=o_recv.at[k],
            device_id={"azim": to},
        )

    def start_out(k, carry):
        send_out(k).start()
        return carry

    lax.fori_loop(1, n, start_out, 0)
    own_o = pltpu.make_async_copy(obuf.at[:, rows(me), :], out.at[:, :, lanes(me)], own_sem.at[0])
    own_o.start()
    own_o.wait()

    def wait_out(k, carry):
        source = lax.rem(me + n - k, n)
        send_out(k).wait_send()
        pltpu.make_async_remote_copy(
            src_ref=obuf.at[:, rows(source), :],
            dst_ref=out.at[:, :, lanes(source)],
            send_sem=o_send.at[k],
            recv_sem=o_recv.at[k],
            device_id={"azim": source},
        ).wait_recv()
        return carry

    lax.fori_loop(1, n, wait_out, 0)


def by_radius(conserved, velocity, viscosity, shifts):
    fields, block, cols = conserved.shape
    n = lax.axis_size("azim")
    heights = cols // shifts.shape[1]
    width = cols // n
    wide = width + 2 * HALO * heights
    azim = n * block
    f32 = jnp.float32
    dma = pltpu.SemaphoreType.DMA
    return pl.pallas_call(
        functools.partial(disc_kernel, n, heights),
        out_shape=jax.ShapeDtypeStruct(conserved.shape, f32),
        in_specs=[
            pl.BlockSpec(memory_space=pl.ANY),
            pl.BlockSpec(memory_space=pl.ANY),
            pl.BlockSpec(memory_space=pltpu.SMEM),
            pl.BlockSpec(memory_space=pltpu.SMEM),
        ],
        out_specs=pl.BlockSpec(memory_space=pl.ANY),
        scratch_shapes=[
            pltpu.VMEM((fields + 1, azim, width), f32),
            pltpu.VMEM((STEPS, fields + 1, wide, azim), f32),
            pltpu.VMEM((wide, azim), f32),
            pltpu.VMEM((wide, azim), f32),
            pltpu.VMEM((wide, azim), f32),
            pltpu.VMEM((wide, azim), f32),
            pltpu.VMEM((fields, azim, width), f32),
            dma((n,)),
            dma((n,)),
            dma((n,)),
            dma((n,)),
            dma((STEPS, 2)),
            dma((STEPS, 2)),
            dma((n,)),
            dma((n,)),
            dma((2,)),
        ],
        compiler_params=pltpu.CompilerParams(collective_id=0, has_side_effects=True),
    )(conserved, velocity, viscosity, shifts)


def local(conserved, velocity, viscosity, shifts):
    fields, block, cols = conserved.shape
    n = lax.axis_size("azim")
    heights = cols // shifts.shape[1]
    fits = (
        n * block == LANES
        and cols % n == 0
        and cols // n == LANES
        and block % SUBLANES == 0
        and heights % SUBLANES == 0
        and LANES % heights == 0
        and LANES // heights >= HALO
    )
    if fits:
        return by_radius(conserved, velocity, viscosity, shifts)
    return by_azimuth(conserved, velocity, viscosity, shifts)


def solution(mesh):
    in_specs = (
        P(None, ("groups", "azim"), None),
        P(("groups", "azim"), None),
        P(),
        P("groups", None),
    )
    out_specs = P(None, ("groups", "azim"), None)
    return jax.shard_map(local, mesh=mesh, in_specs=in_specs, out_specs=out_specs, check_vma=False)
```

```python
import functools

import jax
import jax.numpy as jnp
from jax import lax
from jax.experimental import pallas as pl
from jax.experimental.pallas import tpu as pltpu
from jax.sharding import PartitionSpec as P

STEPS = 2
HALO = 3
LANES = 128
SUBLANES = 8


def padded(cells, sides, width):
    for axis, dim in sides:
        count = lax.axis_size(axis)
        head = lax.slice_in_dim(cells, 0, width, axis=dim)
        tail = lax.slice_in_dim(cells, cells.shape[dim] - width, cells.shape[dim], axis=dim)
        cells = jnp.concatenate(
            [
                lax.ppermute(tail, axis, [(i, (i + 1) % count) for i in range(count)]),
                cells,
                lax.ppermute(head, axis, [((i + 1) % count, i) for i in range(count)]),
            ],
            axis=dim,
        )
    return cells


def shifted(value, axis, steps):
    count = lax.axis_size(axis)
    pairs = [(source, (source + steps) % count) for source in range(count)]
    return lax.ppermute(value, axis, pairs)


def minmod(left, right):
    return 0.5 * (jnp.sign(left) + jnp.sign(right)) * jnp.minimum(jnp.abs(left), jnp.abs(right))


def lateral_sum(inner, heights):
    width = inner.shape[2]
    height_of = jnp.arange(width, dtype=jnp.int32) % heights
    outward = jnp.concatenate([inner[:, :, heights:], inner[:, :, width - heights :]], axis=2)
    inward = jnp.concatenate([inner[:, :, :heights], inner[:, :, : width - heights]], axis=2)
    upper = jnp.concatenate([inner[:, :, 1:], inner[:, :, width - 1 :]], axis=2)
    upper = jnp.where((height_of == heights - 1)[None, None, :], inner, upper)
    lower = jnp.concatenate([inner[:, :, :1], inner[:, :, : width - 1]], axis=2)
    lower = jnp.where((height_of == 0)[None, None, :], inner, lower)
    return outward + inward + upper + lower - 4.0 * inner


def tendency(ext, speed, viscosity, heights):
    count = ext.shape[1]
    diff = ext[:, 1:] - ext[:, :-1]
    slope = minmod(diff[:, :-1], diff[:, 1:])
    left_state = ext[:, 1 : count - 2] + 0.5 * slope[:, 0 : count - 3]
    right_state = ext[:, 2 : count - 1] - 0.5 * slope[:, 1 : count - 2]
    face_speed = 0.5 * (speed[1 : count - 2] + speed[2 : count - 1])
    flux = jnp.maximum(face_speed, 0.0) * left_state + jnp.minimum(face_speed, 0.0) * right_state
    inner = ext[:, 2 : count - 2]
    azimuthal = ext[:, 3 : count - 1] + ext[:, 1 : count - 3] - 2.0 * inner
    lateral = lateral_sum(inner, heights)
    return -(flux[:, 1:] - flux[:, :-1]) + viscosity[:, None, None] * (azimuthal + lateral)


def section_rim(field):
    return padded(field, (("azim", 1),), 2)


def slide_down(joined, amount, limit):
    current = joined
    level = 0
    while 1 << level < limit:
        stride = 1 << level
        taken = amount >> level & 1 == 1
        moved = jnp.concatenate(
            [jnp.zeros_like(current[:, :stride]), current[:, : current.shape[1] - stride]], axis=1
        )
        current = jnp.where(taken[None, None, :], moved, current)
        level = level + 1
    return current


def by_azimuth(conserved, velocity, viscosity, shifts):
    state = conserved
    block = state.shape[1]
    heights = state.shape[2] // shifts.shape[1]
    devices = lax.axis_size("azim")
    levels = devices.bit_length() - 1
    speed_wide = padded(velocity, (("azim", 0),), 6)
    speed_near = speed_wide[4:-4]
    for step in range(STEPS):
        first = state + tendency(section_rim(state), speed_near, viscosity, heights)
        second = 0.75 * state + 0.25 * (
            first + tendency(section_rim(first), speed_near, viscosity, heights)
        )
        third = 1.0 / 3.0 * state + 2.0 / 3.0 * (
            second + tendency(section_rim(second), speed_near, viscosity, heights)
        )
        per_column = jnp.repeat(shifts[step], heights)
        whole_blocks = per_column // block
        remainder = per_column - whole_blocks * block
        moved = third
        for level in range(levels):
            taken = whole_blocks >> level & 1 == 1
            arrived = shifted(moved, "azim", 1 << level)
            moved = jnp.where(taken[None, None, :], arrived, moved)
        preceding = shifted(moved, "azim", 1)
        joined = jnp.concatenate([preceding, moved], axis=1)
        state = slide_down(joined, remainder, block)[:, block:]
    return state


def winding(d):
    row, chip, core = d // 4, (d % 4) // 2, d % 2
    return row * 4 + ((row + chip) % 2) * 2 + core


def disc_kernel(
    n,
    heights,
    cons,
    vel,
    visc,
    shifts,
    out,
    ubuf,
    u,
    vp,
    vn,
    t1,
    t2,
    obuf,
    a_send,
    a_recv,
    a_own,
    h_send,
    h_recv,
    o_send,
    o_recv,
    o_own,
):
    fields, block, cols = cons.shape
    width = cols // n
    owned = width // heights
    azim = n * block
    rim = HALO * heights
    me = lax.axis_index("azim")
    place = winding(me)
    inward = winding(lax.rem(place + n - 1, n))
    outward = winding(lax.rem(place + 1, n))

    barrier = pltpu.get_barrier_semaphore()

    def greet(k, carry):
        pl.semaphore_signal(barrier, inc=1, device_id={"azim": lax.rem(me + k, n)})
        return carry

    lax.fori_loop(1, n, greet, 0)
    pl.semaphore_wait(barrier, n - 1)

    def lanes(d):
        return pl.ds(pl.multiple_of(d * width, width), width)

    def rows(d):
        return pl.ds(pl.multiple_of(d * block, block), block)

    def share(f, d):
        return vel.at[:, lanes(winding(d))] if f is None else cons.at[f, :, lanes(winding(d))]

    def send_in(f):
        plane = fields if f is None else f

        def one(k, carry):
            to = lax.rem(me + k, n)
            pltpu.make_async_remote_copy(
                src_ref=share(f, to),
                dst_ref=ubuf.at[plane, rows(me), :],
                send_sem=a_send.at[plane],
                recv_sem=a_recv.at[plane],
                device_id={"azim": to},
            ).start()
            return carry

        lax.fori_loop(1, n, one, 0)
        pltpu.make_async_copy(share(f, me), ubuf.at[plane, rows(me), :], a_own.at[plane]).start()

    def all_in(plane):
        others = ubuf.at[plane, pl.ds(0, azim - block), :]
        return pltpu.make_async_remote_copy(
            src_ref=others,
            dst_ref=others,
            send_sem=a_send.at[plane],
            recv_sem=a_recv.at[plane],
            device_id={"azim": outward},
        )

    def halo(step, plane):
        inner = pltpu.make_async_remote_copy(
            src_ref=u.at[step, plane, pl.ds(rim, rim), :],
            dst_ref=u.at[step, plane, pl.ds(rim + width, rim), :],
            send_sem=h_send.at[step, 0, plane],
            recv_sem=h_recv.at[step, 0, plane],
            device_id={"azim": inward},
        )
        outer = pltpu.make_async_remote_copy(
            src_ref=u.at[step, plane, pl.ds(width, rim), :],
            dst_ref=u.at[step, plane, pl.ds(0, rim), :],
            send_sem=h_send.at[step, 1, plane],
            recv_sem=h_recv.at[step, 1, plane],
            device_id={"azim": outward},
        )
        return inner, outer

    def halo_start(step, plane):
        inner, outer = halo(step, plane)
        pl.when(place > 0)(inner.start)
        pl.when(place < n - 1)(outer.start)

    def halo_recv(step, plane):
        inner, outer = halo(step, plane)
        pl.when(place > 0)(outer.wait_recv)
        pl.when(place < n - 1)(inner.wait_recv)

    def halo_sent(step, plane):
        inner, outer = halo(step, plane)
        pl.when(place > 0)(inner.wait_send)
        pl.when(place < n - 1)(outer.wait_send)

    def arrive(plane):
        pltpu.make_async_copy(
            ubuf.at[plane, rows(me), :], ubuf.at[plane, rows(me), :], a_own.at[plane]
        ).wait()
        all_in(plane).wait_recv()
        u[0, plane, rim : rim + width, :] = ubuf[plane].T
        halo_start(0, plane)

    def send_out(f):
        def one(k, carry):
            to = lax.rem(me + k, n)
            pltpu.make_async_remote_copy(
                src_ref=obuf.at[f, rows(to), :],
                dst_ref=out.at[f, :, lanes(place)],
                send_sem=o_send.at[f],
                recv_sem=o_recv.at[f],
                device_id={"azim": to},
            ).start()
            return carry

        lax.fori_loop(1, n, one, 0)
        pltpu.make_async_copy(obuf.at[f, rows(me), :], out.at[f, :, lanes(place)], o_own.at[f]).start()

    top = lax.broadcasted_iota(jnp.int32, (heights, azim), 0) == heights - 1
    radii = owned + 2 * HALO

    def part(r):
        return slice(r * heights, (r + 1) * heights)

    def stage(load, nu, first, last, write):
        here = load(first)
        below = here - load(first - 1)
        if first == HALO:
            below = jnp.where(place == 0, 0.0, below)
        for r in range(first, last):
            after = load(r + 1)
            above = after - here
            if r + 1 == HALO:
                above = jnp.where(place == 0, 0.0, above)
            if r + 1 == HALO + owned:
                above = jnp.where(place == n - 1, 0.0, above)
            x = here
            d = x - pltpu.roll(x, 1, 1)
            dp = pltpu.roll(d, azim - 1, 1)
            low = jnp.minimum(d, dp)
            high = jnp.maximum(d, dp)
            half = 0.5 * (jnp.maximum(low, 0.0) + jnp.minimum(high, 0.0))
            p = vp[part(r), :] * (x + half)
            q = vn[part(r), :] * (x - half)
            change = (p - q) + (pltpu.roll(q, azim - 1, 1) - pltpu.roll(p, 1, 1))
            e = jnp.where(top, 0.0, pltpu.roll(x, heights - 1, 0) - x)
            spread = (dp - d) + (e - pltpu.roll(e, 1, 0)) + (above - below)
            write(r, x, nu * spread - change)
            here = after
            below = above

    def advance(step, f):
        nu = visc[f]

        def write1(r, x, change):
            t1[part(r), :] = x + change

        def write2(r, x, change):
            t2[part(r), :] = 0.75 * u[step, f, part(r), :] + 0.25 * (x + change)

        def write3(r, x, change):
            y = (1.0 / 3.0) * u[step, f, part(r), :] + (2.0 / 3.0) * (x + change)
            amount = shifts[step, place * owned + (r - HALO)]
            y = pltpu.roll(y, amount, 1)
            if step + 1 < STEPS:
                u[step + 1, f, part(r), :] = y
            else:
                t1[part(r), :] = y

        stage(lambda r: u[step, f, part(r), :], nu, 1, radii - 1, write1)
        stage(lambda r: t1[part(r), :], nu, 2, radii - 2, write2)
        stage(lambda r: t2[part(r), :], nu, 3, radii - 3, write3)

    def each(body, count=fields):
        def one(f, carry):
            body(f)
            return carry

        lax.fori_loop(0, count, one, 0)

    send_in(None)
    each(send_in)
    arrive(fields)
    arrive(0)
    halo_recv(0, fields)
    for r in range(1, radii - 1):
        v = u[0, fields, part(r), :]
        speed = 0.5 * (v + pltpu.roll(v, 1, 1))
        vn[part(r), :] = jnp.minimum(speed, 0.0)
        vp[part(r), :] = pltpu.roll(jnp.maximum(speed, 0.0), azim - 1, 1)

    for step in range(STEPS):

        def work(f):
            if step == 0:

                @pl.when(f + 1 < fields)
                def _():
                    arrive(f + 1)

            halo_recv(step, f)
            advance(step, f)
            if step + 1 < STEPS:
                halo_start(step + 1, f)
            else:
                obuf[f] = t1[rim : rim + width, :].T
                send_out(f)

        each(work)

    def sent(plane):
        all_in(plane).wait_send()
        halo_sent(0, plane)

    each(sent, fields + 1)

    def finish(f):
        for step in range(1, STEPS):
            halo_sent(step, f)
        pltpu.make_async_copy(
            obuf.at[f, rows(me), :], out.at[f, :, lanes(place)], o_own.at[f]
        ).wait()
        others = obuf.at[f, pl.ds(0, azim - block), :]
        done = pltpu.make_async_remote_copy(
            src_ref=others,
            dst_ref=others,
            send_sem=o_send.at[f],
            recv_sem=o_recv.at[f],
            device_id={"azim": outward},
        )
        done.wait_send()
        done.wait_recv()

    each(finish)


def by_radius(conserved, velocity, viscosity, shifts):
    fields, block, cols = conserved.shape
    n = lax.axis_size("azim")
    heights = cols // shifts.shape[1]
    width = cols // n
    wide = width + 2 * HALO * heights
    azim = n * block
    f32 = jnp.float32
    dma = pltpu.SemaphoreType.DMA
    return pl.pallas_call(
        functools.partial(disc_kernel, n, heights),
        out_shape=jax.ShapeDtypeStruct(conserved.shape, f32),
        in_specs=[
            pl.BlockSpec(memory_space=pl.ANY),
            pl.BlockSpec(memory_space=pl.ANY),
            pl.BlockSpec(memory_space=pltpu.SMEM),
            pl.BlockSpec(memory_space=pltpu.SMEM),
        ],
        out_specs=pl.BlockSpec(memory_space=pl.ANY),
        scratch_shapes=[
            pltpu.VMEM((fields + 1, azim, width), f32),
            pltpu.VMEM((STEPS, fields + 1, wide, azim), f32),
            pltpu.VMEM((wide, azim), f32),
            pltpu.VMEM((wide, azim), f32),
            pltpu.VMEM((wide, azim), f32),
            pltpu.VMEM((wide, azim), f32),
            pltpu.VMEM((fields, azim, width), f32),
            dma((fields + 1,)),
            dma((fields + 1,)),
            dma((fields + 1,)),
            dma((STEPS, 2, fields + 1)),
            dma((STEPS, 2, fields + 1)),
            dma((fields,)),
            dma((fields,)),
            dma((fields,)),
        ],
        compiler_params=pltpu.CompilerParams(collective_id=0, has_side_effects=True),
    )(conserved, velocity, viscosity, shifts)


def local(conserved, velocity, viscosity, shifts):
    fields, block, cols = conserved.shape
    n = lax.axis_size("azim")
    heights = cols // shifts.shape[1]
    fits = (
        n % 8 == 0
        and n * block == LANES
        and cols % n == 0
        and cols // n == LANES
        and block % SUBLANES == 0
        and heights % SUBLANES == 0
        and LANES % heights == 0
        and LANES // heights >= HALO
    )
    if fits:
        return by_radius(conserved, velocity, viscosity, shifts)
    return by_azimuth(conserved, velocity, viscosity, shifts)


def solution(mesh):
    in_specs = (
        P(None, ("groups", "azim"), None),
        P(("groups", "azim"), None),
        P(),
        P("groups", None),
    )
    out_specs = P(None, ("groups", "azim"), None)
    return jax.shard_map(local, mesh=mesh, in_specs=in_specs, out_specs=out_specs, check_vma=False)
```

```python
import functools

import jax
import jax.numpy as jnp
from jax import lax
from jax.experimental import pallas as pl
from jax.experimental.pallas import tpu as pltpu
from jax.sharding import PartitionSpec as P

STEPS = 2
HALO = 3
LANES = 128
SUBLANES = 8


def padded(cells, sides, width):
    for axis, dim in sides:
        count = lax.axis_size(axis)
        head = lax.slice_in_dim(cells, 0, width, axis=dim)
        tail = lax.slice_in_dim(cells, cells.shape[dim] - width, cells.shape[dim], axis=dim)
        cells = jnp.concatenate(
            [
                lax.ppermute(tail, axis, [(i, (i + 1) % count) for i in range(count)]),
                cells,
                lax.ppermute(head, axis, [((i + 1) % count, i) for i in range(count)]),
            ],
            axis=dim,
        )
    return cells


def shifted(value, axis, steps):
    count = lax.axis_size(axis)
    pairs = [(source, (source + steps) % count) for source in range(count)]
    return lax.ppermute(value, axis, pairs)


def minmod(left, right):
    return 0.5 * (jnp.sign(left) + jnp.sign(right)) * jnp.minimum(jnp.abs(left), jnp.abs(right))


def lateral_sum(inner, heights):
    width = inner.shape[2]
    height_of = jnp.arange(width, dtype=jnp.int32) % heights
    outward = jnp.concatenate([inner[:, :, heights:], inner[:, :, width - heights :]], axis=2)
    inward = jnp.concatenate([inner[:, :, :heights], inner[:, :, : width - heights]], axis=2)
    upper = jnp.concatenate([inner[:, :, 1:], inner[:, :, width - 1 :]], axis=2)
    upper = jnp.where((height_of == heights - 1)[None, None, :], inner, upper)
    lower = jnp.concatenate([inner[:, :, :1], inner[:, :, : width - 1]], axis=2)
    lower = jnp.where((height_of == 0)[None, None, :], inner, lower)
    return outward + inward + upper + lower - 4.0 * inner


def tendency(ext, speed, viscosity, heights):
    count = ext.shape[1]
    diff = ext[:, 1:] - ext[:, :-1]
    slope = minmod(diff[:, :-1], diff[:, 1:])
    left_state = ext[:, 1 : count - 2] + 0.5 * slope[:, 0 : count - 3]
    right_state = ext[:, 2 : count - 1] - 0.5 * slope[:, 1 : count - 2]
    face_speed = 0.5 * (speed[1 : count - 2] + speed[2 : count - 1])
    flux = jnp.maximum(face_speed, 0.0) * left_state + jnp.minimum(face_speed, 0.0) * right_state
    inner = ext[:, 2 : count - 2]
    azimuthal = ext[:, 3 : count - 1] + ext[:, 1 : count - 3] - 2.0 * inner
    lateral = lateral_sum(inner, heights)
    return -(flux[:, 1:] - flux[:, :-1]) + viscosity[:, None, None] * (azimuthal + lateral)


def section_rim(field):
    return padded(field, (("azim", 1),), 2)


def slide_down(joined, amount, limit):
    current = joined
    level = 0
    while 1 << level < limit:
        stride = 1 << level
        taken = amount >> level & 1 == 1
        moved = jnp.concatenate(
            [jnp.zeros_like(current[:, :stride]), current[:, : current.shape[1] - stride]], axis=1
        )
        current = jnp.where(taken[None, None, :], moved, current)
        level = level + 1
    return current


def by_azimuth(conserved, velocity, viscosity, shifts):
    state = conserved
    block = state.shape[1]
    heights = state.shape[2] // shifts.shape[1]
    devices = lax.axis_size("azim")
    levels = devices.bit_length() - 1
    speed_wide = padded(velocity, (("azim", 0),), 6)
    speed_near = speed_wide[4:-4]
    for step in range(STEPS):
        first = state + tendency(section_rim(state), speed_near, viscosity, heights)
        second = 0.75 * state + 0.25 * (
            first + tendency(section_rim(first), speed_near, viscosity, heights)
        )
        third = 1.0 / 3.0 * state + 2.0 / 3.0 * (
            second + tendency(section_rim(second), speed_near, viscosity, heights)
        )
        per_column = jnp.repeat(shifts[step], heights)
        whole_blocks = per_column // block
        remainder = per_column - whole_blocks * block
        moved = third
        for level in range(levels):
            taken = whole_blocks >> level & 1 == 1
            arrived = shifted(moved, "azim", 1 << level)
            moved = jnp.where(taken[None, None, :], arrived, moved)
        preceding = shifted(moved, "azim", 1)
        joined = jnp.concatenate([preceding, moved], axis=1)
        state = slide_down(joined, remainder, block)[:, block:]
    return state


def winding(d):
    row, chip, core = d // 4, (d % 4) // 2, d % 2
    return row * 4 + ((row + chip) % 2) * 2 + core


def disc_kernel(
    n,
    heights,
    cons,
    vel,
    visc_in,
    shifts_in,
    out,
    visc,
    shifts,
    s_own,
    ubuf,
    u,
    vp,
    vn,
    t1,
    t2,
    obuf,
    a_send,
    a_recv,
    a_own,
    h_send,
    h_recv,
    o_send,
    o_recv,
    o_own,
    xbuf,
    x_send,
    x_recv,
    x_own,
):
    fields, block, cols = cons.shape
    width = cols // n
    owned = width // heights
    azim = n * block
    rim = HALO * heights
    me = lax.axis_index("azim")
    place = winding(me)
    inward = winding(lax.rem(place + n - 1, n))
    outward = winding(lax.rem(place + 1, n))
    middle = n // 2

    barrier = pltpu.get_barrier_semaphore()

    def greet(k, carry):
        pl.semaphore_signal(barrier, inc=1, device_id={"azim": lax.rem(me + k, n)})
        return carry

    lax.fori_loop(1, n, greet, 0)
    pl.semaphore_wait(barrier, n - 1)

    def lanes(d):
        return pl.ds(pl.multiple_of(d * width, width), width)

    def rows(d):
        return pl.ds(pl.multiple_of(d * block, block), block)

    def share(f, d):
        return vel.at[:, lanes(winding(d))] if f is None else cons.at[f, :, lanes(winding(d))]

    def send_in(f):
        plane = fields if f is None else f

        def one(k, carry):
            to = lax.rem(me + k, n)
            pltpu.make_async_remote_copy(
                src_ref=share(f, to),
                dst_ref=ubuf.at[plane, rows(me), :],
                send_sem=a_send.at[plane],
                recv_sem=a_recv.at[plane],
                device_id={"azim": to},
            ).start()
            return carry

        lax.fori_loop(1, n, one, 0)
        pltpu.make_async_copy(share(f, me), ubuf.at[plane, rows(me), :], a_own.at[plane]).start()
        for taker, giver in ((middle - 1, middle), (middle, middle - 1)):

            @pl.when(place != taker)
            def _():
                pltpu.make_async_remote_copy(
                    src_ref=share(f, winding(giver)),
                    dst_ref=xbuf.at[plane, rows(me), :],
                    send_sem=x_send.at[plane],
                    recv_sem=x_recv.at[plane],
                    device_id={"azim": winding(taker)},
                ).start()

            @pl.when(place == taker)
            def _():
                pltpu.make_async_copy(
                    share(f, winding(giver)), xbuf.at[plane, rows(me), :], x_own.at[plane]
                ).start()

    def cross(plane, count):
        others = xbuf.at[plane, pl.ds(0, count * block), :]
        return pltpu.make_async_remote_copy(
            src_ref=others,
            dst_ref=others,
            send_sem=x_send.at[plane],
            recv_sem=x_recv.at[plane],
            device_id={"azim": outward},
        )

    def cross_in(plane):
        pltpu.make_async_copy(
            xbuf.at[plane, rows(me), :], xbuf.at[plane, rows(me), :], x_own.at[plane]
        ).wait()
        cross(plane, n - 1).wait_recv()
        return xbuf[plane].T

    def linked(step):
        if step == 0:
            return (place > 0) & (place != middle), (place < n - 1) & (place != middle - 1)
        return place > 0, place < n - 1

    def all_in(plane):
        others = ubuf.at[plane, pl.ds(0, azim - block), :]
        return pltpu.make_async_remote_copy(
            src_ref=others,
            dst_ref=others,
            send_sem=a_send.at[plane],
            recv_sem=a_recv.at[plane],
            device_id={"azim": outward},
        )

    def halo(step, plane):
        inner = pltpu.make_async_remote_copy(
            src_ref=u.at[step, plane, pl.ds(rim, rim), :],
            dst_ref=u.at[step, plane, pl.ds(rim + width, rim), :],
            send_sem=h_send.at[step, 0, plane],
            recv_sem=h_recv.at[step, 0, plane],
            device_id={"azim": inward},
        )
        outer = pltpu.make_async_remote_copy(
            src_ref=u.at[step, plane, pl.ds(width, rim), :],
            dst_ref=u.at[step, plane, pl.ds(0, rim), :],
            send_sem=h_send.at[step, 1, plane],
            recv_sem=h_recv.at[step, 1, plane],
            device_id={"azim": outward},
        )
        return inner, outer

    def halo_start(step, plane):
        inner, outer = halo(step, plane)
        back, ahead = linked(step)
        pl.when(back)(inner.start)
        pl.when(ahead)(outer.start)

    def halo_recv(step, plane):
        inner, outer = halo(step, plane)
        back, ahead = linked(step)
        pl.when(back)(outer.wait_recv)
        pl.when(ahead)(inner.wait_recv)

    def halo_sent(step, plane):
        inner, outer = halo(step, plane)
        back, ahead = linked(step)
        pl.when(back)(inner.wait_send)
        pl.when(ahead)(outer.wait_send)

    def arrive(plane):
        pltpu.make_async_copy(
            ubuf.at[plane, rows(me), :], ubuf.at[plane, rows(me), :], a_own.at[plane]
        ).wait()
        all_in(plane).wait_recv()
        u[0, plane, rim : rim + width, :] = ubuf[plane].T
        halo_start(0, plane)

        @pl.when(place == middle - 1)
        def _():
            u[0, plane, rim + width : rim + width + rim, :] = cross_in(plane)[:rim]

        @pl.when(place == middle)
        def _():
            u[0, plane, 0:rim, :] = cross_in(plane)[width - rim :]

    def send_out(f):
        def one(k, carry):
            to = lax.rem(me + k, n)
            pltpu.make_async_remote_copy(
                src_ref=obuf.at[f, rows(to), :],
                dst_ref=out.at[f, :, lanes(place)],
                send_sem=o_send.at[f],
                recv_sem=o_recv.at[f],
                device_id={"azim": to},
            ).start()
            return carry

        lax.fori_loop(1, n, one, 0)
        pltpu.make_async_copy(obuf.at[f, rows(me), :], out.at[f, :, lanes(place)], o_own.at[f]).start()

    top = lax.broadcasted_iota(jnp.int32, (heights, azim), 0) == heights - 1
    radii = owned + 2 * HALO

    def part(r):
        return slice(r * heights, (r + 1) * heights)

    def stage(load, nu, first, last, write):
        here = load(first)
        below = here - load(first - 1)
        if first == HALO:
            below = jnp.where(place == 0, 0.0, below)
        for r in range(first, last):
            after = load(r + 1)
            above = after - here
            if r + 1 == HALO:
                above = jnp.where(place == 0, 0.0, above)
            if r + 1 == HALO + owned:
                above = jnp.where(place == n - 1, 0.0, above)
            x = here
            d = x - pltpu.roll(x, 1, 1)
            dp = pltpu.roll(d, azim - 1, 1)
            low = jnp.minimum(d, dp)
            high = jnp.maximum(d, dp)
            half = 0.5 * (jnp.maximum(low, 0.0) + jnp.minimum(high, 0.0))
            p = vp[part(r), :] * (x + half)
            q = vn[part(r), :] * (x - half)
            change = (p - q) + (pltpu.roll(q, azim - 1, 1) - pltpu.roll(p, 1, 1))
            e = jnp.where(top, 0.0, pltpu.roll(x, heights - 1, 0) - x)
            spread = (dp - d) + (e - pltpu.roll(e, 1, 0)) + (above - below)
            write(r, x, nu * spread - change)
            here = after
            below = above

    def advance(step, f):
        nu = visc[f]

        def write1(r, x, change):
            t1[part(r), :] = x + change

        def write2(r, x, change):
            t2[part(r), :] = 0.75 * u[step, f, part(r), :] + 0.25 * (x + change)

        def write3(r, x, change):
            y = (1.0 / 3.0) * u[step, f, part(r), :] + (2.0 / 3.0) * (x + change)
            amount = shifts[step, place * owned + (r - HALO)]
            y = pltpu.roll(y, amount, 1)
            if step + 1 < STEPS:
                u[step + 1, f, part(r), :] = y
            else:
                t1[part(r), :] = y

        stage(lambda r: u[step, f, part(r), :], nu, 1, radii - 1, write1)
        stage(lambda r: t1[part(r), :], nu, 2, radii - 2, write2)
        stage(lambda r: t2[part(r), :], nu, 3, radii - 3, write3)

    def each(body, count=fields):
        def one(f, carry):
            body(f)
            return carry

        lax.fori_loop(0, count, one, 0)

    scalars = (
        pltpu.make_async_copy(visc_in, visc, s_own.at[0]),
        pltpu.make_async_copy(shifts_in, shifts, s_own.at[1]),
    )
    for copy in scalars:
        copy.start()
    send_in(None)
    each(send_in)
    arrive(fields)
    arrive(0)
    for copy in scalars:
        copy.wait()
    halo_recv(0, fields)
    for r in range(1, radii - 1):
        v = u[0, fields, part(r), :]
        speed = 0.5 * (v + pltpu.roll(v, 1, 1))
        vn[part(r), :] = jnp.minimum(speed, 0.0)
        vp[part(r), :] = pltpu.roll(jnp.maximum(speed, 0.0), azim - 1, 1)

    for step in range(STEPS):

        def work(f):
            if step == 0:

                @pl.when(f + 1 < fields)
                def _():
                    arrive(f + 1)

            halo_recv(step, f)
            advance(step, f)
            if step + 1 < STEPS:
                halo_start(step + 1, f)
            else:
                obuf[f] = t1[rim : rim + width, :].T
                send_out(f)

        each(work)

    def sent(plane):
        all_in(plane).wait_send()
        at_middle = (place == middle - 1) | (place == middle)
        pl.when(at_middle)(cross(plane, 1).wait_send)
        pl.when(jnp.logical_not(at_middle))(cross(plane, 2).wait_send)
        halo_sent(0, plane)

    each(sent, fields + 1)

    def finish(f):
        for step in range(1, STEPS):
            halo_sent(step, f)
        pltpu.make_async_copy(
            obuf.at[f, rows(me), :], out.at[f, :, lanes(place)], o_own.at[f]
        ).wait()
        others = obuf.at[f, pl.ds(0, azim - block), :]
        done = pltpu.make_async_remote_copy(
            src_ref=others,
            dst_ref=others,
            send_sem=o_send.at[f],
            recv_sem=o_recv.at[f],
            device_id={"azim": outward},
        )
        done.wait_send()
        done.wait_recv()

    each(finish)


def by_radius(conserved, velocity, viscosity, shifts):
    fields, block, cols = conserved.shape
    n = lax.axis_size("azim")
    heights = cols // shifts.shape[1]
    width = cols // n
    wide = width + 2 * HALO * heights
    azim = n * block
    f32 = jnp.float32
    dma = pltpu.SemaphoreType.DMA
    return pl.pallas_call(
        functools.partial(disc_kernel, n, heights),
        out_shape=jax.ShapeDtypeStruct(conserved.shape, f32),
        in_specs=[
            pl.BlockSpec(memory_space=pl.ANY),
            pl.BlockSpec(memory_space=pl.ANY),
            pl.BlockSpec(memory_space=pl.ANY),
            pl.BlockSpec(memory_space=pl.ANY),
        ],
        out_specs=pl.BlockSpec(memory_space=pl.ANY),
        scratch_shapes=[
            pltpu.SMEM(viscosity.shape, f32),
            pltpu.SMEM(shifts.shape, jnp.int32),
            dma((2,)),
            pltpu.VMEM((fields + 1, azim, width), f32),
            pltpu.VMEM((STEPS, fields + 1, wide, azim), f32),
            pltpu.VMEM((wide, azim), f32),
            pltpu.VMEM((wide, azim), f32),
            pltpu.VMEM((wide, azim), f32),
            pltpu.VMEM((wide, azim), f32),
            pltpu.VMEM((fields, azim, width), f32),
            dma((fields + 1,)),
            dma((fields + 1,)),
            dma((fields + 1,)),
            dma((STEPS, 2, fields + 1)),
            dma((STEPS, 2, fields + 1)),
            dma((fields,)),
            dma((fields,)),
            dma((fields,)),
            pltpu.VMEM((fields + 1, azim, width), f32),
            dma((fields + 1,)),
            dma((fields + 1,)),
            dma((fields + 1,)),
        ],
        compiler_params=pltpu.CompilerParams(collective_id=0, has_side_effects=True),
    )(conserved, velocity, viscosity, shifts)


def local(conserved, velocity, viscosity, shifts):
    fields, block, cols = conserved.shape
    n = lax.axis_size("azim")
    heights = cols // shifts.shape[1]
    fits = (
        n % 8 == 0
        and n * block == LANES
        and cols % n == 0
        and cols // n == LANES
        and block % SUBLANES == 0
        and heights % SUBLANES == 0
        and LANES % heights == 0
        and LANES // heights >= HALO
    )
    if fits:
        return by_radius(conserved, velocity, viscosity, shifts)
    return by_azimuth(conserved, velocity, viscosity, shifts)


def solution(mesh):
    in_specs = (
        P(None, ("groups", "azim"), None),
        P(("groups", "azim"), None),
        P(),
        P("groups", None),
    )
    out_specs = P(None, ("groups", "azim"), None)
    return jax.shard_map(local, mesh=mesh, in_specs=in_specs, out_specs=out_specs, check_vma=False)
```

```python
import functools

import jax
import jax.numpy as jnp
from jax import lax
from jax.experimental import pallas as pl
from jax.experimental.pallas import tpu as pltpu
from jax.sharding import PartitionSpec as P

STEPS = 2
HALO = 3
LANES = 128
SUBLANES = 8


def padded(cells, sides, width):
    for axis, dim in sides:
        count = lax.axis_size(axis)
        head = lax.slice_in_dim(cells, 0, width, axis=dim)
        tail = lax.slice_in_dim(cells, cells.shape[dim] - width, cells.shape[dim], axis=dim)
        cells = jnp.concatenate(
            [
                lax.ppermute(tail, axis, [(i, (i + 1) % count) for i in range(count)]),
                cells,
                lax.ppermute(head, axis, [((i + 1) % count, i) for i in range(count)]),
            ],
            axis=dim,
        )
    return cells


def shifted(value, axis, steps):
    count = lax.axis_size(axis)
    pairs = [(source, (source + steps) % count) for source in range(count)]
    return lax.ppermute(value, axis, pairs)


def minmod(left, right):
    return 0.5 * (jnp.sign(left) + jnp.sign(right)) * jnp.minimum(jnp.abs(left), jnp.abs(right))


def lateral_sum(inner, heights):
    width = inner.shape[2]
    height_of = jnp.arange(width, dtype=jnp.int32) % heights
    outward = jnp.concatenate([inner[:, :, heights:], inner[:, :, width - heights :]], axis=2)
    inward = jnp.concatenate([inner[:, :, :heights], inner[:, :, : width - heights]], axis=2)
    upper = jnp.concatenate([inner[:, :, 1:], inner[:, :, width - 1 :]], axis=2)
    upper = jnp.where((height_of == heights - 1)[None, None, :], inner, upper)
    lower = jnp.concatenate([inner[:, :, :1], inner[:, :, : width - 1]], axis=2)
    lower = jnp.where((height_of == 0)[None, None, :], inner, lower)
    return outward + inward + upper + lower - 4.0 * inner


def tendency(ext, speed, viscosity, heights):
    count = ext.shape[1]
    diff = ext[:, 1:] - ext[:, :-1]
    slope = minmod(diff[:, :-1], diff[:, 1:])
    left_state = ext[:, 1 : count - 2] + 0.5 * slope[:, 0 : count - 3]
    right_state = ext[:, 2 : count - 1] - 0.5 * slope[:, 1 : count - 2]
    face_speed = 0.5 * (speed[1 : count - 2] + speed[2 : count - 1])
    flux = jnp.maximum(face_speed, 0.0) * left_state + jnp.minimum(face_speed, 0.0) * right_state
    inner = ext[:, 2 : count - 2]
    azimuthal = ext[:, 3 : count - 1] + ext[:, 1 : count - 3] - 2.0 * inner
    lateral = lateral_sum(inner, heights)
    return -(flux[:, 1:] - flux[:, :-1]) + viscosity[:, None, None] * (azimuthal + lateral)


def section_rim(field):
    return padded(field, (("azim", 1),), 2)


def slide_down(joined, amount, limit):
    current = joined
    level = 0
    while 1 << level < limit:
        stride = 1 << level
        taken = amount >> level & 1 == 1
        moved = jnp.concatenate(
            [jnp.zeros_like(current[:, :stride]), current[:, : current.shape[1] - stride]], axis=1
        )
        current = jnp.where(taken[None, None, :], moved, current)
        level = level + 1
    return current


def by_azimuth(conserved, velocity, viscosity, shifts):
    state = conserved
    block = state.shape[1]
    heights = state.shape[2] // shifts.shape[1]
    devices = lax.axis_size("azim")
    levels = devices.bit_length() - 1
    speed_wide = padded(velocity, (("azim", 0),), 6)
    speed_near = speed_wide[4:-4]
    for step in range(STEPS):
        first = state + tendency(section_rim(state), speed_near, viscosity, heights)
        second = 0.75 * state + 0.25 * (
            first + tendency(section_rim(first), speed_near, viscosity, heights)
        )
        third = 1.0 / 3.0 * state + 2.0 / 3.0 * (
            second + tendency(section_rim(second), speed_near, viscosity, heights)
        )
        per_column = jnp.repeat(shifts[step], heights)
        whole_blocks = per_column // block
        remainder = per_column - whole_blocks * block
        moved = third
        for level in range(levels):
            taken = whole_blocks >> level & 1 == 1
            arrived = shifted(moved, "azim", 1 << level)
            moved = jnp.where(taken[None, None, :], arrived, moved)
        preceding = shifted(moved, "azim", 1)
        joined = jnp.concatenate([preceding, moved], axis=1)
        state = slide_down(joined, remainder, block)[:, block:]
    return state


def winding(d):
    row, chip, core = d // 4, (d % 4) // 2, d % 2
    return row * 4 + ((row + chip) % 2) * 2 + core


def disc_kernel(
    n,
    heights,
    cons,
    vel,
    visc_in,
    shifts_in,
    out,
    visc,
    shifts,
    s_own,
    ubuf,
    u,
    vp,
    vn,
    t1,
    t2,
    obuf,
    a_send,
    a_recv,
    a_own,
    h_send,
    h_recv,
    o_send,
    o_recv,
    o_own,
    xbuf,
    x_send,
    x_recv,
    x_own,
):
    fields, block, cols = cons.shape
    width = cols // n
    owned = width // heights
    azim = n * block
    rim = HALO * heights
    me = lax.axis_index("azim")
    place = winding(me)
    inward = winding(lax.rem(place + n - 1, n))
    outward = winding(lax.rem(place + 1, n))
    middle = n // 2

    barrier = pltpu.get_barrier_semaphore()

    def greet(k, carry):
        pl.semaphore_signal(barrier, inc=1, device_id={"azim": lax.rem(me + k, n)})
        return carry

    lax.fori_loop(1, n, greet, 0)
    pl.semaphore_wait(barrier, n - 1)

    def lanes(d):
        return pl.ds(pl.multiple_of(d * width, width), width)

    def rows(d):
        return pl.ds(pl.multiple_of(d * block, block), block)

    def share(f, d):
        return vel.at[:, lanes(winding(d))] if f is None else cons.at[f, :, lanes(winding(d))]

    def send_in(f):
        plane = fields if f is None else f

        def one(k, carry):
            to = lax.rem(me + k, n)
            pltpu.make_async_remote_copy(
                src_ref=share(f, to),
                dst_ref=ubuf.at[plane, rows(me), :],
                send_sem=a_send.at[plane],
                recv_sem=a_recv.at[plane],
                device_id={"azim": to},
            ).start()
            return carry

        lax.fori_loop(1, n, one, 0)
        pltpu.make_async_copy(share(f, me), ubuf.at[plane, rows(me), :], a_own.at[plane]).start()
        for taker, giver in ((middle - 1, middle), (middle, middle - 1)):

            @pl.when(place != taker)
            def _():
                pltpu.make_async_remote_copy(
                    src_ref=share(f, winding(giver)),
                    dst_ref=xbuf.at[plane, rows(me), :],
                    send_sem=x_send.at[plane],
                    recv_sem=x_recv.at[plane],
                    device_id={"azim": winding(taker)},
                ).start()

            @pl.when(place == taker)
            def _():
                pltpu.make_async_copy(
                    share(f, winding(giver)), xbuf.at[plane, rows(me), :], x_own.at[plane]
                ).start()

    def cross(plane, count):
        others = xbuf.at[plane, pl.ds(0, count * block), :]
        return pltpu.make_async_remote_copy(
            src_ref=others,
            dst_ref=others,
            send_sem=x_send.at[plane],
            recv_sem=x_recv.at[plane],
            device_id={"azim": outward},
        )

    def cross_in(plane):
        pltpu.make_async_copy(
            xbuf.at[plane, rows(me), :], xbuf.at[plane, rows(me), :], x_own.at[plane]
        ).wait()
        cross(plane, n - 1).wait_recv()
        return xbuf[plane].T

    def linked(step):
        if step == 0:
            return (place > 0) & (place != middle), (place < n - 1) & (place != middle - 1)
        return place > 0, place < n - 1

    def all_in(plane):
        others = ubuf.at[plane, pl.ds(0, azim - block), :]
        return pltpu.make_async_remote_copy(
            src_ref=others,
            dst_ref=others,
            send_sem=a_send.at[plane],
            recv_sem=a_recv.at[plane],
            device_id={"azim": outward},
        )

    def halo(step, plane):
        inner = pltpu.make_async_remote_copy(
            src_ref=u.at[step, plane, pl.ds(rim, rim), :],
            dst_ref=u.at[step, plane, pl.ds(rim + width, rim), :],
            send_sem=h_send.at[step, 0, plane],
            recv_sem=h_recv.at[step, 0, plane],
            device_id={"azim": inward},
        )
        outer = pltpu.make_async_remote_copy(
            src_ref=u.at[step, plane, pl.ds(width, rim), :],
            dst_ref=u.at[step, plane, pl.ds(0, rim), :],
            send_sem=h_send.at[step, 1, plane],
            recv_sem=h_recv.at[step, 1, plane],
            device_id={"azim": outward},
        )
        return inner, outer

    def halo_start(step, plane):
        inner, outer = halo(step, plane)
        back, ahead = linked(step)
        pl.when(back)(inner.start)
        pl.when(ahead)(outer.start)

    def halo_recv(step, plane):
        inner, outer = halo(step, plane)
        back, ahead = linked(step)
        pl.when(back)(outer.wait_recv)
        pl.when(ahead)(inner.wait_recv)

    def halo_sent(step, plane):
        inner, outer = halo(step, plane)
        back, ahead = linked(step)
        pl.when(back)(inner.wait_send)
        pl.when(ahead)(outer.wait_send)

    def arrive(plane):
        pltpu.make_async_copy(
            ubuf.at[plane, rows(me), :], ubuf.at[plane, rows(me), :], a_own.at[plane]
        ).wait()
        all_in(plane).wait_recv()
        u[0, plane, rim : rim + width, :] = ubuf[plane].T
        halo_start(0, plane)

        @pl.when(place == middle - 1)
        def _():
            u[0, plane, rim + width : rim + width + rim, :] = cross_in(plane)[:rim]

        @pl.when(place == middle)
        def _():
            u[0, plane, 0:rim, :] = cross_in(plane)[width - rim :]

    def send_out(f):
        def one(k, carry):
            to = lax.rem(me + k, n)
            pltpu.make_async_remote_copy(
                src_ref=obuf.at[f, rows(to), :],
                dst_ref=out.at[f, :, lanes(place)],
                send_sem=o_send.at[f],
                recv_sem=o_recv.at[f],
                device_id={"azim": to},
            ).start()
            return carry

        lax.fori_loop(1, n, one, 0)
        pltpu.make_async_copy(obuf.at[f, rows(me), :], out.at[f, :, lanes(place)], o_own.at[f]).start()

    top = lax.broadcasted_iota(jnp.int32, (heights, azim), 0) == heights - 1
    radii = owned + 2 * HALO

    def part(r):
        return slice(r * heights, (r + 1) * heights)

    def stage(load, nu, first, last, write):
        here = load(first)
        below = here - load(first - 1)
        if first == HALO:
            below = jnp.where(place == 0, 0.0, below)
        for r in range(first, last):
            after = load(r + 1)
            above = after - here
            if r + 1 == HALO:
                above = jnp.where(place == 0, 0.0, above)
            if r + 1 == HALO + owned:
                above = jnp.where(place == n - 1, 0.0, above)
            x = here
            d = x - pltpu.roll(x, 1, 1)
            dp = pltpu.roll(d, azim - 1, 1)
            low = jnp.minimum(d, dp)
            high = jnp.maximum(d, dp)
            half = 0.5 * (jnp.maximum(low, 0.0) + jnp.minimum(high, 0.0))
            p = vp[part(r), :] * (x + half)
            q = vn[part(r), :] * (x - half)
            change = (p - q) + (pltpu.roll(q, azim - 1, 1) - pltpu.roll(p, 1, 1))
            e = jnp.where(top, 0.0, pltpu.roll(x, heights - 1, 0) - x)
            spread = (dp - d) + (e - pltpu.roll(e, 1, 0)) + (above - below)
            write(r, x, nu * spread - change)
            here = after
            below = above

    def advance(step, f):
        nu = visc[f]

        def write1(r, x, change):
            t1[part(r), :] = x + change

        def write2(r, x, change):
            t2[part(r), :] = 0.75 * u[step, f, part(r), :] + 0.25 * (x + change)

        def write3(r, x, change):
            y = (1.0 / 3.0) * u[step, f, part(r), :] + (2.0 / 3.0) * (x + change)
            amount = shifts[step, place * owned + (r - HALO)]
            y = pltpu.roll(y, amount, 1)
            if step + 1 < STEPS:
                u[step + 1, f, part(r), :] = y
            else:
                t1[part(r), :] = y

        stage(lambda r: u[step, f, part(r), :], nu, 1, radii - 1, write1)
        stage(lambda r: t1[part(r), :], nu, 2, radii - 2, write2)
        stage(lambda r: t2[part(r), :], nu, 3, radii - 3, write3)

    def each(body, count=fields):
        def one(f, carry):
            body(f)
            return carry

        lax.fori_loop(0, count, one, 0)

    scalars = (
        pltpu.make_async_copy(visc_in, visc, s_own.at[0]),
        pltpu.make_async_copy(shifts_in, shifts, s_own.at[1]),
    )
    for copy in scalars:
        copy.start()
    send_in(None)
    each(send_in)
    arrive(fields)
    arrive(0)
    arrive(1)
    for copy in scalars:
        copy.wait()
    halo_recv(0, fields)
    for r in range(1, radii - 1):
        v = u[0, fields, part(r), :]
        speed = 0.5 * (v + pltpu.roll(v, 1, 1))
        vn[part(r), :] = jnp.minimum(speed, 0.0)
        vp[part(r), :] = pltpu.roll(jnp.maximum(speed, 0.0), azim - 1, 1)

    for step in range(STEPS):

        def work(f):
            if step == 0:

                @pl.when(f + 2 < fields)
                def _():
                    arrive(f + 2)

            halo_recv(step, f)
            advance(step, f)
            if step + 1 < STEPS:
                halo_start(step + 1, f)
            else:
                obuf[f] = t1[rim : rim + width, :].T
                send_out(f)

        each(work)

    def sent(plane):
        all_in(plane).wait_send()
        at_middle = (place == middle - 1) | (place == middle)
        pl.when(at_middle)(cross(plane, 1).wait_send)
        pl.when(jnp.logical_not(at_middle))(cross(plane, 2).wait_send)
        halo_sent(0, plane)

    each(sent, fields + 1)

    def finish(f):
        for step in range(1, STEPS):
            halo_sent(step, f)
        pltpu.make_async_copy(
            obuf.at[f, rows(me), :], out.at[f, :, lanes(place)], o_own.at[f]
        ).wait()
        others = obuf.at[f, pl.ds(0, azim - block), :]
        done = pltpu.make_async_remote_copy(
            src_ref=others,
            dst_ref=others,
            send_sem=o_send.at[f],
            recv_sem=o_recv.at[f],
            device_id={"azim": outward},
        )
        done.wait_send()
        done.wait_recv()

    each(finish)


def by_radius(conserved, velocity, viscosity, shifts):
    fields, block, cols = conserved.shape
    n = lax.axis_size("azim")
    heights = cols // shifts.shape[1]
    width = cols // n
    wide = width + 2 * HALO * heights
    azim = n * block
    f32 = jnp.float32
    dma = pltpu.SemaphoreType.DMA
    return pl.pallas_call(
        functools.partial(disc_kernel, n, heights),
        out_shape=jax.ShapeDtypeStruct(conserved.shape, f32),
        in_specs=[
            pl.BlockSpec(memory_space=pl.ANY),
            pl.BlockSpec(memory_space=pl.ANY),
            pl.BlockSpec(memory_space=pl.ANY),
            pl.BlockSpec(memory_space=pl.ANY),
        ],
        out_specs=pl.BlockSpec(memory_space=pl.ANY),
        scratch_shapes=[
            pltpu.SMEM(viscosity.shape, f32),
            pltpu.SMEM(shifts.shape, jnp.int32),
            dma((2,)),
            pltpu.VMEM((fields + 1, azim, width), f32),
            pltpu.VMEM((STEPS, fields + 1, wide, azim), f32),
            pltpu.VMEM((wide, azim), f32),
            pltpu.VMEM((wide, azim), f32),
            pltpu.VMEM((wide, azim), f32),
            pltpu.VMEM((wide, azim), f32),
            pltpu.VMEM((fields, azim, width), f32),
            dma((fields + 1,)),
            dma((fields + 1,)),
            dma((fields + 1,)),
            dma((STEPS, 2, fields + 1)),
            dma((STEPS, 2, fields + 1)),
            dma((fields,)),
            dma((fields,)),
            dma((fields,)),
            pltpu.VMEM((fields + 1, azim, width), f32),
            dma((fields + 1,)),
            dma((fields + 1,)),
            dma((fields + 1,)),
        ],
        compiler_params=pltpu.CompilerParams(collective_id=0, has_side_effects=True),
    )(conserved, velocity, viscosity, shifts)


def local(conserved, velocity, viscosity, shifts):
    fields, block, cols = conserved.shape
    n = lax.axis_size("azim")
    heights = cols // shifts.shape[1]
    fits = (
        n % 8 == 0
        and n * block == LANES
        and cols % n == 0
        and cols // n == LANES
        and block % SUBLANES == 0
        and heights % SUBLANES == 0
        and LANES % heights == 0
        and LANES // heights >= HALO
    )
    if fits:
        return by_radius(conserved, velocity, viscosity, shifts)
    return by_azimuth(conserved, velocity, viscosity, shifts)


def solution(mesh):
    in_specs = (
        P(None, ("groups", "azim"), None),
        P(("groups", "azim"), None),
        P(),
        P("groups", None),
    )
    out_specs = P(None, ("groups", "azim"), None)
    return jax.shard_map(local, mesh=mesh, in_specs=in_specs, out_specs=out_specs, check_vma=False)
```
